512 devices in a mesh: seq: 16 (over y_lo, x, core), head: 32 (over z, y_hi).
Axes of the slice: x: 4, y: 8 (y_hi: 4, y_lo: 2; y = y_hi * 2 + y_lo), z: 8, core: 2. Of those that a mesh axis runs over, the one named last changes fastest.
Arguments:
- queries: bfloat16 [2048, 8192], P('seq', 'head'), may hold values from -256 to 256
- key_rows: bfloat16 [2048, 128], P('seq'), may hold values from -6 to 6
- value_rows: bfloat16 [2048, 128], P('seq'), may hold values from -6 to 6
- pair_keys: bfloat16 [2048, 128], P('seq'), may hold values from 0.27 to 1.73
- pair_values: bfloat16 [2048, 128], P('seq'), may hold values from 0.099609375 to 1.8984375
- first_key: int32 [2048], P('seq'), may hold values from 0 to 2047, as said below
- residual: float32 [2048, 8192], P(('seq', 'head')), may hold values from -6 to 6
- out_weight: bfloat16 [8192, 8192], P('head', 'seq'), may hold values from -0.25 to 0.25
Outputs:
- updated: float32 [2048, 8192], P(('seq', 'head'))
The draws below stay inside these ranges and needn't reach their ends.
Inputs may be any that keep to these rules, and one draw needn't show every extreme that they name: first_key never falls along the tokens, first_key[i] <= i, and first_key[i] = i where a document begins; positions 0 and 2047 begin one.
All inputs are finite; a program needn't handle non-finite values.
Results may differ from the reference program's by a relative error of at most 0.005.
Values may be sent and summed in bfloat16 or wider, within the bound.
A program may use at most 64 MiB of HBM per device.

```python
import math
import jax
import jax.numpy as jnp
from jax import lax

D = 8192
HEADS = 64
DH = 128
W1 = 512
W2 = 32
TOKENS = 2048


def drawn_draw(key):
    base_key = jax.random.fold_in(key, 5)
    key_first, key_second, key_third = jax.random.split(base_key, 3)
    key_table = jnp.clip(jax.random.normal(key_first, (TOKENS, DH), jnp.float32), -6.0, 6.0)
    pair_table = 1.0 + 0.18 * jnp.clip(jax.random.normal(key_second, (TOKENS, DH), jnp.float32), -4.0, 4.0)
    query_table = jnp.clip(jax.random.normal(key_third, (TOKENS, HEADS, DH), jnp.float32), -6.0, 6.0)
    return (query_table.reshape(TOKENS, HEADS * DH), key_table, pair_table)


def draw_queries(key, part):
    return drawn_draw(key)[0].astype(jnp.bfloat16)


def draw_key_rows(key, part):
    return drawn_draw(key)[1].astype(jnp.bfloat16)


def draw_pair_keys(key, part):
    return drawn_draw(key)[2].astype(jnp.bfloat16)


def draw_first_key(key, part):
    count_starts = max(2, TOKENS // 256)
    start_rows = jax.random.randint(jax.random.fold_in(key, 11), (count_starts,), 1, TOKENS)
    flags = jnp.zeros((TOKENS,), jnp.int32).at[start_rows].set(1).at[0].set(1).at[TOKENS - 1].set(1)
    positions = jnp.arange(TOKENS, dtype=jnp.int32)
    return lax.cummax(jnp.where(flags > 0, positions, 0), axis=0)


def level_of(key, extent, cuts, least, high):
    def one(axis_at, parts):
        heights = jax.random.uniform(jax.random.fold_in(jax.random.fold_in(key, 6), axis_at), (parts,), jnp.float32, least / len(cuts), high / len(cuts))
        return jnp.repeat(jnp.exp(heights), extent[axis_at] // parts).reshape((-1,) + (1,) * (len(extent) - axis_at - 1))

    factor_of = one(*cuts[0])
    for cut in cuts[1:]:
        factor_of = factor_of * one(*cut)
    return factor_of


def normal_values(stream_key, extent, deviation, bound, shards=(), kind=jnp.bfloat16):
    result = jax.random.normal(stream_key, extent, jnp.float32) * deviation
    if len(shards) > 0:
        result = level_of(stream_key, extent, shards, -0.22, 0.18) * result
    return jnp.clip(result, min=-bound, max=bound).astype(kind)


def setup_inputs(seed: int = 0) -> dict:
    arg_keys = jax.random.split(jax.random.key(seed), 9)
    return {
        "queries": draw_queries(jax.random.fold_in(arg_keys[8], 71), 0),
        "key_rows": draw_key_rows(jax.random.fold_in(arg_keys[8], 71), 0),
        "value_rows": normal_values(arg_keys[2], (TOKENS, DH), 1.0, 6.0, ((0, 16),)),
        "pair_keys": draw_pair_keys(jax.random.fold_in(arg_keys[8], 71), 0),
        "pair_values": jnp.clip(1.0 + 0.18 * jax.random.normal(arg_keys[4], (TOKENS, DH), jnp.float32), 0.099609375, 1.8984375).astype(jnp.bfloat16),
        "first_key": draw_first_key(jax.random.fold_in(arg_keys[8], 71), 0),
        "residual": normal_values(arg_keys[6], (TOKENS, D), 1.0, 6.0, ((0, 512),), jnp.float32),
        "out_weight": normal_values(arg_keys[7], (HEADS * DH, D), (HEADS * DH // 16) ** -0.5, 0.25, ((0, 32), (1, 16))),
    }


MASKED_SCORE = -1e+30

def reference(queries, key_rows, value_rows, pair_keys, pair_values, first_key, residual, out_weight):
    scale_factor = 1.0 / math.sqrt(DH)
    qblock = 16
    key_padded = jnp.concatenate([jnp.zeros((W1, DH), key_rows.dtype), key_rows], axis=0)
    value_padded = jnp.concatenate([jnp.zeros((W1, DH), value_rows.dtype), value_rows], axis=0)
    pair_key_padded = jnp.concatenate([jnp.zeros((W2, DH), pair_keys.dtype), pair_keys], axis=0)
    pair_value_padded = jnp.concatenate([jnp.zeros((W2, DH), pair_values.dtype), pair_values], axis=0)
    unfold_index = (jnp.arange(TOKENS, dtype=jnp.int32)[:, None] + 1 + jnp.arange(W2, dtype=jnp.int32)[None, :]).astype(jnp.int32)
    pair_key_win = pair_key_padded[unfold_index]
    pair_value_win = pair_value_padded[unfold_index]
    query_heads = queries.reshape(TOKENS, HEADS, DH)

    def attend(row_start):
        query_blk = lax.dynamic_slice_in_dim(query_heads, row_start, qblock, 0).astype(jnp.float32)
        pair_kblk = lax.dynamic_slice_in_dim(pair_key_win, row_start, qblock, 0).astype(jnp.float32)
        pair_vblk = lax.dynamic_slice_in_dim(pair_value_win, row_start, qblock, 0).astype(jnp.float32)
        pair_mix = (query_blk[:, :, None, :] * pair_kblk[:, None, :, :]).astype(jnp.bfloat16)
        key_blk = lax.dynamic_slice_in_dim(key_padded, row_start, W1 + qblock, 0).astype(jnp.float32)
        value_blk = lax.dynamic_slice_in_dim(value_padded, row_start, W1 + qblock, 0).astype(jnp.float32)
        logits = jnp.einsum('ahod,kd->ahok', pair_mix.astype(jnp.float32), key_blk) * scale_factor
        query_pos = row_start + jnp.arange(qblock, dtype=jnp.int32)
        key_pos = row_start - W1 + jnp.arange(W1 + qblock, dtype=jnp.int32)
        pair_pos = query_pos[:, None] - W2 + 1 + jnp.arange(W2, dtype=jnp.int32)[None, :]
        lower_bound = lax.dynamic_slice_in_dim(first_key, row_start, qblock, 0)
        key_ok = (key_pos[None, :] <= query_pos[:, None]) & (key_pos[None, :] > query_pos[:, None] - W1) & (key_pos[None, :] >= lower_bound[:, None])
        pair_ok = pair_pos >= lower_bound[:, None]
        allowed = key_ok[:, None, None, :] & pair_ok[:, None, :, None]
        logits = jnp.where(allowed, logits, MASKED_SCORE)
        row_top = lax.optimization_barrier(jnp.max(logits, axis=(2, 3), keepdims=True))
        expo = jnp.where(allowed, jnp.exp(logits - row_top), 0.0)
        row_total = lax.optimization_barrier(jnp.sum(expo, axis=(2, 3), keepdims=True))
        rounded_weight = (expo / row_total).astype(jnp.bfloat16)
        carried = jnp.einsum('ahok,kd->ahod', rounded_weight.astype(jnp.float32), value_blk)
        return lax.optimization_barrier(jnp.sum(carried * pair_vblk[:, None, :, :], axis=2)).astype(jnp.bfloat16)
    starts = jnp.arange(TOKENS // qblock, dtype=jnp.int32) * qblock
    attended = lax.map(attend, starts).reshape(TOKENS, HEADS * DH)
    return residual + jnp.dot(attended, out_weight, preferred_element_type=jnp.float32)
```

```python
import functools
import math

import jax
import jax.numpy as jnp
from jax import lax
from jax.experimental import pallas as pl
from jax.experimental.pallas import tpu as pltpu
from jax.sharding import PartitionSpec as P

DH = 128
W1 = 512
W2 = 32
TOK = 128
HL = 2
KSPAN = W1 + TOK
NX = 4
NZ = 8
NY = 4
NC = 8
BIG = -1e30
MESH = pl.DeviceIdType.MESH
F32 = jnp.float32
BF16 = jnp.bfloat16
SUB = 8


def kernel(
    q_ref, k_ref, v_ref, pk_ref, pv_ref, fkrow_ref, fks_ref, w_ref, out_ref,
    rhs, vaug, pkc, pvc, pkf, pvf, qf, lhs, prob, att, abuf, wf,
    rsend, rown, rrecv, ffin, fsend, frecv,
    hs, hr, w1s, w1r, w2s, w2r, w3s, w3r, a_s, a_r, rs_s, rs_r, f_s, f_r,
):
    s = lax.axis_index("seq")
    h = lax.axis_index("head")
    z = h // NY
    yh = h % NY
    core = s % 2
    c = s // 2
    x = c % NX
    yl = c // NX
    base = s * TOK

    def dev(seq, head):
        return {"seq": seq, "head": head}

    def rcopy(src, dst, ssem, rsem, seq, head):
        return pltpu.make_async_remote_copy(
            src_ref=src, dst_ref=dst, send_sem=ssem, recv_sem=rsem,
            device_id=dev(seq, head), device_id_type=MESH,
        )

    bar = pltpu.get_barrier_semaphore()
    count = 0
    for k in range(1, 16):
        pl.semaphore_signal(bar, inc=1, device_id=dev((s + k) % 16, h), device_id_type=MESH)
        count += 1
    for k in range(1, NZ):
        for dc in range(2):
            pl.semaphore_signal(
                bar, inc=1, device_id=dev(c * 2 + (core + dc) % 2, ((z + k) % NZ) * NY + yh),
                device_id_type=MESH)
            count += 1
    for k in range(1, NY):
        pl.semaphore_signal(bar, inc=1, device_id=dev(s, z * NY + (yh + k) % NY), device_id_type=MESH)
        count += 1
    pl.semaphore_wait(bar, count)

    def halo(o):
        rows = pl.ds((4 - o) * TOK, TOK)
        res = [
            rcopy(k_ref, rhs.at[rows, pl.ds(0, DH)], hs.at[o, 0], hr.at[o, 0], (s + o) % 16, h),
            rcopy(v_ref, vaug.at[rows, pl.ds(0, DH)], hs.at[o, 1], hr.at[o, 1], (s + o) % 16, h),
        ]
        if o == 1:
            tail = pl.ds(TOK - W2, W2)
            head = pl.ds(0, W2)
            res.append(rcopy(pk_ref.at[tail], pkc.at[head], hs.at[0, 0], hr.at[0, 0], (s + 1) % 16, h))
            res.append(rcopy(pv_ref.at[tail], pvc.at[head], hs.at[0, 1], hr.at[0, 1], (s + 1) % 16, h))
        return res

    for o in range(1, 5):
        @pl.when(s + o < 16)
        def _():
            for cp in halo(o):
                cp.start()

    ki = z % 2
    wi = z // 2

    def w1_copy(q):
        src = w_ref.at[:, pl.ds(q * 128, 128)]
        dst = wf.at[ki, c, wi]
        return src, dst, 4 * core + q

    for q in range(4):
        src, dst, zd = w1_copy(q)
        mine = (zd == z) & (ki == core)

        @pl.when(mine)
        def _():
            pltpu.make_async_copy(src, dst, w1r.at[wi]).start()

        @pl.when(jnp.logical_not(mine))
        def _():
            rcopy(src, dst, w1s.at[q], w1r.at[wi], c * 2 + ki, zd * NY + yh).start()

    rhs[pl.ds(W1, TOK), pl.ds(0, DH)] = k_ref[...]
    vaug[pl.ds(W1, TOK), pl.ds(0, DH)] = v_ref[...]
    vaug[:, pl.ds(DH, DH)] = jnp.ones((KSPAN, DH), BF16)
    for hd in range(HL):
        qf[hd] = q_ref[:, hd * DH:(hd + 1) * DH].astype(F32)
    pkf[pl.ds(W2, TOK), :] = pk_ref[...].astype(F32)
    pvf[pl.ds(W2, TOK), :] = pv_ref[...].astype(F32)
    for o in range(1, 5):
        @pl.when(s < o)
        def _():
            rhs[pl.ds((4 - o) * TOK, TOK), pl.ds(0, DH)] = jnp.zeros((TOK, DH), BF16)
            vaug[pl.ds((4 - o) * TOK, TOK), pl.ds(0, DH)] = jnp.zeros((TOK, DH), BF16)
            if o == 1:
                pkc[...] = jnp.zeros((W2, DH), BF16)
                pvc[...] = jnp.zeros((W2, DH), BF16)

    for o in range(1, 5):
        @pl.when(s >= o)
        def _():
            for cp in halo(o):
                cp.wait_recv()

    pkf[pl.ds(0, W2), :] = pkc[...].astype(F32)
    pvf[pl.ds(0, W2), :] = pvc[...].astype(F32)

    scale = math.log2(math.e) / math.sqrt(DH)
    lane = lax.broadcasted_iota(jnp.int32, (W2, DH), 1)
    orow = lax.broadcasted_iota(jnp.int32, (W2, DH), 0)

    def a_copy(n, kz):
        rows = pl.ds(n * 32, 32)
        return rcopy(
            abuf.at[z, rows], abuf.at[z, rows], a_s.at[n, kz], a_r.at[n, kz],
            s, ((z + kz) % NZ) * NY + yh)

    def attend(n):
        y = (yh + 1 + n) % NY
        tstar = 4 * ((y + 1) % NY)
        u = lax.broadcasted_iota(jnp.int32, (KSPAN, DH), 0)
        t = lax.broadcasted_iota(jnp.int32, (KSPAN, DH), 1)
        low = jnp.maximum(t + 1, fkrow_ref[...] - base + W1)
        ok = (u >= low) & (u <= t + W1) & (t != tstar)
        rhs[:, pl.ds(DH, DH)] = jnp.where(ok, 0.0, BIG).astype(BF16)

        def sub(i, carry):
            for j in range(SUB):
                tok = 16 * (2 * i + j // 4) + 4 * y + j % 4
                win = pkf[pl.ds(tok + 1, W2), :]
                bad = fks_ref[tok] - (base + tok) + (W2 - 1)
                hot = jnp.where((lane == tok) | ((lane == tstar) & (orow < bad)), 1.0, 0.0).astype(BF16)
                for hd in range(HL):
                    row = (j * HL + hd) * W2
                    qrow = qf[hd, pl.ds(tok, 1), :]
                    lhs[pl.ds(row, W2), pl.ds(0, DH)] = (win * qrow).astype(BF16)
                    lhs[pl.ds(row, W2), pl.ds(DH, DH)] = hot
            sc = lax.dot_general(
                lhs[...], rhs[...], (((1,), (1,)), ((), ())), preferred_element_type=F32)
            for g in range(SUB * HL):
                part = sc[g * W2:(g + 1) * W2]
                top = part[:, 0:128]
                for b in range(1, 5):
                    top = jnp.maximum(top, part[:, b * 128:(b + 1) * 128])
                top = jnp.maximum(jnp.maximum(top[0:8], top[8:16]), jnp.maximum(top[16:24], top[24:32]))
                top = jnp.max(jnp.max(top, axis=0, keepdims=True), axis=1, keepdims=True)
                prob[pl.ds(g * W2, W2), :] = jnp.exp2((part - top) * scale).astype(BF16)
            car = jnp.dot(prob[...], vaug[...], preferred_element_type=F32)
            for j in range(SUB):
                tok = 16 * (2 * i + j // 4) + 4 * y + j % 4
                win = pvf[pl.ds(tok + 1, W2), :]
                for hd in range(HL):
                    row = (j * HL + hd) * W2
                    num = car[row:row + W2, 0:DH] * win
                    den = car[row:row + W2, DH:2 * DH]
                    num = (num[0:8] + num[8:16]) + (num[16:24] + num[24:32])
                    den = (den[0:8] + den[8:16]) + (den[16:24] + den[24:32])
                    num = jnp.sum(num, axis=0, keepdims=True)
                    den = jnp.sum(den, axis=0, keepdims=True)
                    att[hd, pl.ds(i * SUB + j, 1), :] = num / den
            return carry

        lax.fori_loop(0, 32 // SUB, sub, 0)
        for hd in range(HL):
            abuf[z, pl.ds(n * 32, 32), pl.ds(hd * DH, DH)] = att[hd].astype(BF16)
        for kz in range(1, NZ):
            a_copy(n, kz).start()

    def chip(d):
        return ((yl + d // NX) % 2) * NX + (x + d % NX) % NX

    def chip_from(d):
        return ((yl + d // NX) % 2) * NX + (x + NX - d % NX) % NX

    def w2_copy(d, i):
        return rcopy(wf.at[core, c, i], wf.at[core, c, i], w2s.at[d, i], w2r.at[d, i], chip(d) * 2 + core, h)

    def w3_copy(d):
        blk = wf.at[core, chip_from(d)]
        return rcopy(blk, blk, w3s.at[d], w3r.at[d], c * 2 + (core + 1) % 2, h)

    attend(0)
    for i in range(4):
        pltpu.make_async_copy(wf.at[core, c, i], wf.at[core, c, i], w1r.at[i]).wait()
        for d in range(1, NC):
            w2_copy(d, i).start()
    w3_copy(0).start()
    for n in range(1, 4):
        attend(n)

    for n in range(4):
        for kz in range(1, NZ):
            a_copy(n, kz).wait_recv()

    def rs_copy(n, pair):
        return rcopy(
            rsend.at[n, pair], rrecv.at[n, pair], rs_s.at[n, pair], rs_r.at[n, pair],
            s, z * NY + (yh + 1 + n) % NY)

    order = (0, 1, 3, 4, 2, 5, 7, 6)
    for pair in range(4):
        ds = order[2 * pair:2 * pair + 2]
        for d in ds:
            if d > 0:
                for i in range(4):
                    w2_copy(d, i).wait_recv()
                w3_copy(d).start()
        for d in ds:
            w3_copy(d).wait_recv()
        acc = None
        for zz in range(NZ):
            rhs_w = jnp.concatenate([wf[zz % 2, chip_from(d), zz // 2] for d in ds], axis=1)
            term = jnp.dot(abuf[zz], rhs_w, preferred_element_type=F32)
            acc = term if acc is None else acc + term
        for n in range(3):
            rsend[n, pair] = acc[n * 32:(n + 1) * 32].astype(BF16)
            rs_copy(n, pair).start()
        rown[pair] = acc[96:128]

    for pair in range(4):
        total = rown[pair]
        for n in range(3):
            rs_copy(n, pair).wait_recv()
            total = total + rrecv[n, pair].astype(F32)
        for e in range(2):
            for zz in range(NZ):
                ffin[zz, pl.ds((2 * pair + e) * 4, 4), :] = total[zz * 4:zz * 4 + 4, e * 128:(e + 1) * 128]
    fsend[...] = ffin[...].astype(BF16)

    def f_copy(kz):
        return rcopy(
            fsend.at[(z + kz) % NZ], frecv.at[kz], f_s.at[kz], f_r.at[kz], s, ((z + kz) % NZ) * NY + yh)

    for kz in range(1, NZ):
        f_copy(kz).start()

    def place(val, zs):
        for e in range(NC):
            col = chip_from(order[e]) * (NZ * 128) + zs * 128
            out_ref[:, pl.ds(pl.multiple_of(col, 128), 128)] = val[e * 4:e * 4 + 4]

    place(ffin[z], z)
    for kz in range(1, NZ):
        f_copy(kz).wait_recv()
        place(frecv[kz].astype(F32), (z + NZ - kz) % NZ)

    for o in range(1, 5):
        @pl.when(s + o < 16)
        def _():
            for cp in halo(o):
                cp.wait_send()
    for q in range(4):
        src, dst, zd = w1_copy(q)

        @pl.when(jnp.logical_not((zd == z) & (ki == core)))
        def _():
            rcopy(src, dst, w1s.at[q], w1r.at[wi], c * 2 + ki, zd * NY + yh).wait_send()
    for d in range(1, NC):
        for i in range(4):
            w2_copy(d, i).wait_send()
    for d in range(NC):
        w3_copy(d).wait_send()
    for n in range(4):
        for kz in range(1, NZ):
            a_copy(n, kz).wait_send()
    for n in range(3):
        for pair in range(4):
            rs_copy(n, pair).wait_send()
    for kz in range(1, NZ):
        f_copy(kz).wait_send()


def local(queries, key_rows, value_rows, pair_keys, pair_values, first_key, residual, out_weight):
    vm = pl.BlockSpec(memory_space=pltpu.VMEM)
    dma = pltpu.SemaphoreType.DMA
    summed = pl.pallas_call(
        kernel,
        out_shape=jax.ShapeDtypeStruct((4, 8192), F32),
        in_specs=[vm, vm, vm, vm, vm, vm, pl.BlockSpec(memory_space=pltpu.SMEM),
                  pl.BlockSpec(memory_space=pl.ANY)],
        out_specs=vm,
        scratch_shapes=[
            pltpu.VMEM((KSPAN, 2 * DH), BF16),
            pltpu.VMEM((KSPAN, 2 * DH), BF16),
            pltpu.VMEM((W2, DH), BF16),
            pltpu.VMEM((W2, DH), BF16),
            pltpu.VMEM((W2 + TOK, DH), F32),
            pltpu.VMEM((W2 + TOK, DH), F32),
            pltpu.VMEM((HL, TOK, DH), F32),
            pltpu.VMEM((SUB * HL * W2, 2 * DH), BF16),
            pltpu.VMEM((SUB * HL * W2, KSPAN), BF16),
            pltpu.VMEM((HL, 32, DH), F32),
            pltpu.VMEM((NZ, TOK, HL * DH), BF16),
            pltpu.VMEM((2, NC, 4, HL * DH, 128), BF16),
            pltpu.VMEM((3, 4, 32, 256), BF16),
            pltpu.VMEM((4, 32, 256), F32),
            pltpu.VMEM((3, 4, 32, 256), BF16),
            pltpu.VMEM((NZ, 32, 128), F32),
            pltpu.VMEM((NZ, 32, 128), BF16),
            pltpu.VMEM((NZ, 32, 128), BF16),
            dma((5, 2)), dma((5, 2)),
            dma((4,)), dma((4,)),
            dma((NC, 4)), dma((NC, 4)),
            dma((NC,)), dma((NC,)),
            dma((4, NZ)), dma((4, NZ)),
            dma((3, 4)), dma((3, 4)),
            dma((NZ,)), dma((NZ,)),
        ],
        compiler_params=pltpu.CompilerParams(collective_id=0, has_side_effects=True),
        name="layer",
    )(queries, key_rows, value_rows, pair_keys, pair_values, first_key.reshape(1, TOK), first_key, out_weight)
    return residual + summed


def solution(mesh):
    placed = (
        P("seq", "head"),
        P("seq", None),
        P("seq", None),
        P("seq", None),
        P("seq", None),
        P("seq"),
        P(("seq", "head"), None),
        P("head", "seq"),
    )
    return jax.shard_map(
        local, mesh=mesh, in_specs=placed, out_specs=P(("seq", "head"), None), check_vma=False
    )
```

```python
import functools
import math

import jax
import jax.numpy as jnp
from jax import lax
from jax.experimental import pallas as pl
from jax.experimental.pallas import tpu as pltpu
from jax.sharding import PartitionSpec as P

DH = 128
W1 = 512
W2 = 32
TOK = 128
HL = 2
KSPAN = W1 + TOK
NX = 4
NZ = 8
NY = 4
NC = 8
BIG = -1e30
MESH = pl.DeviceIdType.MESH
F32 = jnp.float32
BF16 = jnp.bfloat16
SUB = 8


def kernel(
    q_ref, k_ref, v_ref, pk_ref, pv_ref, fkrow_ref, fks_ref, w_ref, out_ref,
    rhs, vaug, pkc, pvc, pkf, pvf, qf, lhs, prob, att, abuf, wf,
    rsend, rown, rrecv, ffin, fsend, frecv,
    hs, hr, w1s, w1r, w2s, w2r, w3s, w3r, a_s, a_r, rs_s, rs_r, f_s, f_r,
):
    s = lax.axis_index("seq")
    h = lax.axis_index("head")
    z = h // NY
    yh = h % NY
    core = s % 2
    c = s // 2
    x = c % NX
    yl = c // NX
    base = s * TOK

    def dev(seq, head):
        return {"seq": seq, "head": head}

    def rcopy(src, dst, ssem, rsem, seq, head):
        return pltpu.make_async_remote_copy(
            src_ref=src, dst_ref=dst, send_sem=ssem, recv_sem=rsem,
            device_id=dev(seq, head), device_id_type=MESH,
        )

    bar = pltpu.get_barrier_semaphore()
    count = 0
    for k in range(1, 16):
        pl.semaphore_signal(bar, inc=1, device_id=dev((s + k) % 16, h), device_id_type=MESH)
        count += 1
    for k in range(1, NZ):
        for dc in range(2):
            pl.semaphore_signal(
                bar, inc=1, device_id=dev(c * 2 + (core + dc) % 2, ((z + k) % NZ) * NY + yh),
                device_id_type=MESH)
            count += 1
    for k in range(1, NY):
        pl.semaphore_signal(bar, inc=1, device_id=dev(s, z * NY + (yh + k) % NY), device_id_type=MESH)
        count += 1
    pl.semaphore_wait(bar, count)

    def halo(o):
        rows = pl.ds((4 - o) * TOK, TOK)
        res = [
            rcopy(k_ref, rhs.at[rows, pl.ds(0, DH)], hs.at[o, 0], hr.at[o, 0], (s + o) % 16, h),
            rcopy(v_ref, vaug.at[rows, pl.ds(0, DH)], hs.at[o, 1], hr.at[o, 1], (s + o) % 16, h),
        ]
        if o == 1:
            tail = pl.ds(TOK - W2, W2)
            head = pl.ds(0, W2)
            res.append(rcopy(pk_ref.at[tail], pkc.at[head], hs.at[0, 0], hr.at[0, 0], (s + 1) % 16, h))
            res.append(rcopy(pv_ref.at[tail], pvc.at[head], hs.at[0, 1], hr.at[0, 1], (s + 1) % 16, h))
        return res

    for o in range(1, 5):
        @pl.when(s + o < 16)
        def _():
            for cp in halo(o):
                cp.start()

    ki = z % 2
    wi = z // 2

    def w1_copy(q):
        src = w_ref.at[:, pl.ds(q * 128, 128)]
        dst = wf.at[ki, c, wi]
        return src, dst, 4 * core + q

    for q in range(4):
        src, dst, zd = w1_copy(q)
        mine = (zd == z) & (ki == core)

        @pl.when(mine)
        def _():
            pltpu.make_async_copy(src, dst, w1r.at[wi]).start()

        @pl.when(jnp.logical_not(mine))
        def _():
            rcopy(src, dst, w1s.at[q], w1r.at[wi], c * 2 + ki, zd * NY + yh).start()

    rhs[pl.ds(W1, TOK), pl.ds(0, DH)] = k_ref[...]
    vaug[pl.ds(W1, TOK), pl.ds(0, DH)] = v_ref[...]
    vaug[:, pl.ds(DH, DH)] = jnp.ones((KSPAN, DH), BF16)
    for hd in range(HL):
        qf[hd] = q_ref[:, hd * DH:(hd + 1) * DH].astype(F32)
    pkf[pl.ds(W2, TOK), :] = pk_ref[...].astype(F32)
    pvf[pl.ds(W2, TOK), :] = pv_ref[...].astype(F32)
    for o in range(1, 5):
        @pl.when(s < o)
        def _():
            rhs[pl.ds((4 - o) * TOK, TOK), pl.ds(0, DH)] = jnp.zeros((TOK, DH), BF16)
            vaug[pl.ds((4 - o) * TOK, TOK), pl.ds(0, DH)] = jnp.zeros((TOK, DH), BF16)
            if o == 1:
                pkc[...] = jnp.zeros((W2, DH), BF16)
                pvc[...] = jnp.zeros((W2, DH), BF16)

    for o in range(1, 5):
        @pl.when(s >= o)
        def _():
            for cp in halo(o):
                cp.wait_recv()

    pkf[pl.ds(0, W2), :] = pkc[...].astype(F32)
    pvf[pl.ds(0, W2), :] = pvc[...].astype(F32)

    scale = math.log2(math.e) / math.sqrt(DH)
    lane = lax.broadcasted_iota(jnp.int32, (W2, DH), 1)
    orow = lax.broadcasted_iota(jnp.int32, (W2, DH), 0)

    def a_copy(n, kz):
        rows = pl.ds(n * 32, 32)
        return rcopy(
            abuf.at[z, rows], abuf.at[z, rows], a_s.at[n, kz], a_r.at[n, kz],
            s, ((z + kz) % NZ) * NY + yh)

    def attend(n):
        y = (yh + 1 + n) % NY
        tstar = 4 * ((y + 1) % NY)
        u = lax.broadcasted_iota(jnp.int32, (KSPAN, DH), 0)
        t = lax.broadcasted_iota(jnp.int32, (KSPAN, DH), 1)
        low = jnp.maximum(t + 1, fkrow_ref[...] - base + W1)
        ok = (u >= low) & (u <= t + W1) & (t != tstar)
        rhs[:, pl.ds(DH, DH)] = jnp.where(ok, 0.0, BIG).astype(BF16)

        def sub(i, carry):
            for j in range(SUB):
                tok = 16 * (2 * i + j // 4) + 4 * y + j % 4
                win = pkf[pl.ds(tok + 1, W2), :]
                bad = fks_ref[tok] - (base + tok) + (W2 - 1)
                hot = jnp.where((lane == tok) | ((lane == tstar) & (orow < bad)), 1.0, 0.0).astype(BF16)
                for hd in range(HL):
                    row = (j * HL + hd) * W2
                    qrow = qf[hd, pl.ds(tok, 1), :]
                    lhs[pl.ds(row, W2), pl.ds(0, DH)] = (win * qrow).astype(BF16)
                    lhs[pl.ds(row, W2), pl.ds(DH, DH)] = hot
            sc = lax.dot_general(
                lhs[...], rhs[...], (((1,), (1,)), ((), ())), preferred_element_type=F32)
            for g in range(SUB * HL):
                part = sc[g * W2:(g + 1) * W2]
                top = part[:, 0:128]
                for b in range(1, 5):
                    top = jnp.maximum(top, part[:, b * 128:(b + 1) * 128])
                top = jnp.maximum(jnp.maximum(top[0:8], top[8:16]), jnp.maximum(top[16:24], top[24:32]))
                top = jnp.max(jnp.max(top, axis=0, keepdims=True), axis=1, keepdims=True)
                prob[pl.ds(g * W2, W2), :] = jnp.exp2((part - top) * scale).astype(BF16)
            car = jnp.dot(prob[...], vaug[...], preferred_element_type=F32)
            for j in range(SUB):
                tok = 16 * (2 * i + j // 4) + 4 * y + j % 4
                win = pvf[pl.ds(tok + 1, W2), :]
                for hd in range(HL):
                    row = (j * HL + hd) * W2
                    num = car[row:row + W2, 0:DH] * win
                    den = car[row:row + W2, DH:2 * DH]
                    num = (num[0:8] + num[8:16]) + (num[16:24] + num[24:32])
                    den = (den[0:8] + den[8:16]) + (den[16:24] + den[24:32])
                    num = jnp.sum(num, axis=0, keepdims=True)
                    den = jnp.sum(den, axis=0, keepdims=True)
                    att[hd, pl.ds(i * SUB + j, 1), :] = num / den
            return carry

        lax.fori_loop(0, 32 // SUB, sub, 0, unroll=True)
        for hd in range(HL):
            abuf[z, pl.ds(n * 32, 32), pl.ds(hd * DH, DH)] = att[hd].astype(BF16)
        for kz in range(1, NZ):
            a_copy(n, kz).start()

    def chip_from(d):
        return ((yl + d // NX) % 2) * NX + (x + NX - d % NX) % NX

    def seq_at(dx, dy):
        return (((yl + dy) % 2) * NX + (x + NX + dx) % NX) * 2 + core

    def w2_send(d, i, to):
        dx, dy = to
        e = ((d // NX + dy) % 2) * NX + (d % NX + dx) % NX
        blk = wf.at[core, chip_from(d), i]
        return rcopy(blk, blk, w2s.at[e, i], w2r.at[e, i], seq_at(dx, dy), h)

    def w2_wait(d, i):
        blk = wf.at[core, chip_from(d), i]
        rcopy(blk, blk, w2s.at[d, i], w2r.at[d, i], seq_at(1, 0), h).wait_recv()

    def w3_copy(d):
        blk = wf.at[core, chip_from(d)]
        return rcopy(blk, blk, w3s.at[d], w3r.at[d], c * 2 + (core + 1) % 2, h)

    right, left, across = (1, 0), (-1, 0), (0, 1)
    relays = (
        (((1, 0), (right,)), ((4, 0), (right, left))),
        (((1, 1), (across,)), ((3, 1), (left,)), ((4, 1), (left,))),
        (((1, 2), (across,)), ((3, 2), (left,)), ((4, 2), (left,)),
         ((1, 3), (across,)), ((3, 3), (left, across)), ((7, 0), (left,))),
        (((7, 1), (left,)), ((2, 2), (across,)), ((2, 3), (across,))),
    )
    seen = set()

    def relay(step):
        for (d, i), targets in relays[step]:
            w2_wait(d, i)
            seen.add((d, i))
            for to in targets:
                w2_send(d, i, to).start()

    for i in range(4):
        pltpu.make_async_copy(wf.at[core, c, i], wf.at[core, c, i], w1r.at[i]).wait()
        for to in (right, left, across):
            w2_send(0, i, to).start()
    w3_copy(0).start()
    for n in range(4):
        attend(n)
        relay(n)
        if n == 2:
            w3_copy(1).start()

    for n in range(4):
        for kz in range(1, NZ):
            a_copy(n, kz).wait_recv()

    def rs_copy(n, pair):
        return rcopy(
            rsend.at[n, pair], rrecv.at[n, pair], rs_s.at[n, pair], rs_r.at[n, pair],
            s, z * NY + (yh + 1 + n) % NY)

    order = (0, 1, 3, 4, 2, 7, 5, 6)
    for pair in range(4):
        ds = order[2 * pair:2 * pair + 2]
        for d in ds:
            if d > 1:
                for i in range(4):
                    if (d, i) not in seen:
                        w2_wait(d, i)
                w3_copy(d).start()
        for d in ds:
            w3_copy(d).wait_recv()
        acc = None
        for zz in range(NZ):
            rhs_w = jnp.concatenate([wf[zz % 2, chip_from(d), zz // 2] for d in ds], axis=1)
            term = jnp.dot(abuf[zz], rhs_w, preferred_element_type=F32)
            acc = term if acc is None else acc + term
        for n in range(3):
            rsend[n, pair] = acc[n * 32:(n + 1) * 32].astype(BF16)
            rs_copy(n, pair).start()
        rown[pair] = acc[96:128]

    for pair in range(4):
        total = rown[pair]
        for n in range(3):
            rs_copy(n, pair).wait_recv()
            total = total + rrecv[n, pair].astype(F32)
        for e in range(2):
            for zz in range(NZ):
                ffin[zz, pl.ds((2 * pair + e) * 4, 4), :] = total[zz * 4:zz * 4 + 4, e * 128:(e + 1) * 128]
    fsend[...] = ffin[...].astype(BF16)

    def f_copy(kz):
        return rcopy(
            fsend.at[(z + kz) % NZ], frecv.at[kz], f_s.at[kz], f_r.at[kz], s, ((z + kz) % NZ) * NY + yh)

    for kz in range(1, NZ):
        f_copy(kz).start()

    def place(val, zs):
        for e in range(NC):
            col = chip_from(order[e]) * (NZ * 128) + zs * 128
            out_ref[:, pl.ds(pl.multiple_of(col, 128), 128)] = val[e * 4:e * 4 + 4]

    place(ffin[z], z)
    for kz in range(1, NZ):
        f_copy(kz).wait_recv()
        place(frecv[kz].astype(F32), (z + NZ - kz) % NZ)

    for o in range(1, 5):
        @pl.when(s + o < 16)
        def _():
            for cp in halo(o):
                cp.wait_send()
    for q in range(4):
        src, dst, zd = w1_copy(q)

        @pl.when(jnp.logical_not((zd == z) & (ki == core)))
        def _():
            rcopy(src, dst, w1s.at[q], w1r.at[wi], c * 2 + ki, zd * NY + yh).wait_send()
    for i in range(4):
        for to in (right, left, across):
            w2_send(0, i, to).wait_send()
    for step in relays:
        for (d, i), targets in step:
            for to in targets:
                w2_send(d, i, to).wait_send()
    for d in range(NC):
        w3_copy(d).wait_send()
    for n in range(4):
        for kz in range(1, NZ):
            a_copy(n, kz).wait_send()
    for n in range(3):
        for pair in range(4):
            rs_copy(n, pair).wait_send()
    for kz in range(1, NZ):
        f_copy(kz).wait_send()


def local(queries, key_rows, value_rows, pair_keys, pair_values, first_key, residual, out_weight):
    vm = pl.BlockSpec(memory_space=pltpu.VMEM)
    dma = pltpu.SemaphoreType.DMA
    summed = pl.pallas_call(
        kernel,
        out_shape=jax.ShapeDtypeStruct((4, 8192), F32),
        in_specs=[vm, vm, vm, vm, vm, vm, pl.BlockSpec(memory_space=pltpu.SMEM),
                  pl.BlockSpec(memory_space=pl.ANY)],
        out_specs=vm,
        scratch_shapes=[
            pltpu.VMEM((KSPAN, 2 * DH), BF16),
            pltpu.VMEM((KSPAN, 2 * DH), BF16),
            pltpu.VMEM((W2, DH), BF16),
            pltpu.VMEM((W2, DH), BF16),
            pltpu.VMEM((W2 + TOK, DH), F32),
            pltpu.VMEM((W2 + TOK, DH), F32),
            pltpu.VMEM((HL, TOK, DH), F32),
            pltpu.VMEM((SUB * HL * W2, 2 * DH), BF16),
            pltpu.VMEM((SUB * HL * W2, KSPAN), BF16),
            pltpu.VMEM((HL, 32, DH), F32),
            pltpu.VMEM((NZ, TOK, HL * DH), BF16),
            pltpu.VMEM((2, NC, 4, HL * DH, 128), BF16),
            pltpu.VMEM((3, 4, 32, 256), BF16),
            pltpu.VMEM((4, 32, 256), F32),
            pltpu.VMEM((3, 4, 32, 256), BF16),
            pltpu.VMEM((NZ, 32, 128), F32),
            pltpu.VMEM((NZ, 32, 128), BF16),
            pltpu.VMEM((NZ, 32, 128), BF16),
            dma((5, 2)), dma((5, 2)),
            dma((4,)), dma((4,)),
            dma((NC, 4)), dma((NC, 4)),
            dma((NC,)), dma((NC,)),
            dma((4, NZ)), dma((4, NZ)),
            dma((3, 4)), dma((3, 4)),
            dma((NZ,)), dma((NZ,)),
        ],
        compiler_params=pltpu.CompilerParams(collective_id=0, has_side_effects=True),
        name="layer",
    )(queries, key_rows, value_rows, pair_keys, pair_values, first_key.reshape(1, TOK), first_key, out_weight)
    return residual + summed


def solution(mesh):
    placed = (
        P("seq", "head"),
        P("seq", None),
        P("seq", None),
        P("seq", None),
        P("seq", None),
        P("seq"),
        P(("seq", "head"), None),
        P("head", "seq"),
    )
    return jax.shard_map(
        local, mesh=mesh, in_specs=placed, out_specs=P(("seq", "head"), None), check_vma=False
    )
```

```python
import functools
import math

import jax
import jax.numpy as jnp
from jax import lax
from jax.experimental import pallas as pl
from jax.experimental.pallas import tpu as pltpu
from jax.sharding import PartitionSpec as P

DH = 128
W1 = 512
W2 = 32
TOK = 128
HL = 2
KSPAN = W1 + TOK
NX = 4
NZ = 8
NY = 4
NC = 8
BIG = -1e30
MESH = pl.DeviceIdType.MESH
F32 = jnp.float32
BF16 = jnp.bfloat16
SUB = 8


def kernel(
    q_ref, k_ref, v_ref, pk_ref, pv_ref, fkrow_ref, fks_ref, w_ref, out_ref,
    rhs, vaug, pkc, pvc, pkf, pvf, qf, lhs, prob, att, abuf, wf,
    ffin, fsend, frecv,
    hs, hr, w1s, w1r, w2s, w2r, w3s, w3r, a_s, a_r, f_s, f_r,
):
    s = lax.axis_index("seq")
    h = lax.axis_index("head")
    z = h // NY
    yh = h % NY
    core = s % 2
    c = s // 2
    x = c % NX
    yl = c // NX
    base = s * TOK

    def dev(seq, head):
        return {"seq": seq, "head": head}

    def rcopy(src, dst, ssem, rsem, seq, head):
        return pltpu.make_async_remote_copy(
            src_ref=src, dst_ref=dst, send_sem=ssem, recv_sem=rsem,
            device_id=dev(seq, head), device_id_type=MESH,
        )

    bar = pltpu.get_barrier_semaphore()
    count = 0
    for k in range(1, 16):
        pl.semaphore_signal(bar, inc=1, device_id=dev((s + k) % 16, h), device_id_type=MESH)
        count += 1
    for k in range(1, NZ):
        for dc in range(2):
            pl.semaphore_signal(
                bar, inc=1, device_id=dev(c * 2 + (core + dc) % 2, ((z + k) % NZ) * NY + yh),
                device_id_type=MESH)
            count += 1
    for k in range(1, NY):
        pl.semaphore_signal(bar, inc=1, device_id=dev(s, z * NY + (yh + k) % NY), device_id_type=MESH)
        count += 1
    pl.semaphore_wait(bar, count)

    def halo(o):
        rows = pl.ds((4 - o) * TOK, TOK)
        res = [
            rcopy(k_ref, rhs.at[rows, pl.ds(0, DH)], hs.at[o, 0], hr.at[o, 0], (s + o) % 16, h),
            rcopy(v_ref, vaug.at[rows, pl.ds(0, DH)], hs.at[o, 1], hr.at[o, 1], (s + o) % 16, h),
        ]
        if o == 1:
            tail = pl.ds(TOK - W2, W2)
            head = pl.ds(0, W2)
            res.append(rcopy(pk_ref.at[tail], pkc.at[head], hs.at[0, 0], hr.at[0, 0], (s + 1) % 16, h))
            res.append(rcopy(pv_ref.at[tail], pvc.at[head], hs.at[0, 1], hr.at[0, 1], (s + 1) % 16, h))
        return res

    for o in range(1, 5):
        @pl.when(s + o < 16)
        def _():
            for cp in halo(o):
                cp.start()

    near = (0, 1, 3, 2)
    ki = z % 2
    wi = z // 2

    def w1_copy(k):
        q = (z + near[k]) % 4
        src = w_ref.at[:, pl.ds(pl.multiple_of(q * 128, 128), 128)]
        dst = wf.at[ki, c, wi]
        return src, dst, 4 * core + q

    for k in range(4):
        src, dst, zd = w1_copy(k)
        mine = (zd == z) & (ki == core)

        @pl.when(mine)
        def _():
            pltpu.make_async_copy(src, dst, w1r.at[wi]).start()

        @pl.when(jnp.logical_not(mine))
        def _():
            rcopy(src, dst, w1s.at[k], w1r.at[wi], c * 2 + ki, zd * NY + yh).start()

    def chip_from(d):
        return ((yl + d // NX) % 2) * NX + (x + NX - d % NX) % NX

    def seq_at(dx, dy):
        return (((yl + dy) % 2) * NX + (x + NX + dx) % NX) * 2 + core

    def w2_send(d, i, to):
        dx, dy = to
        e = ((d // NX + dy) % 2) * NX + (d % NX + dx) % NX
        blk = wf.at[core, chip_from(d), (wi + near[i]) % 4]
        return rcopy(blk, blk, w2s.at[e, i], w2r.at[e, i], seq_at(dx, dy), h)

    def w2_wait(d, i):
        blk = wf.at[core, chip_from(d), (wi + near[i]) % 4]
        rcopy(blk, blk, w2s.at[d, i], w2r.at[d, i], seq_at(1, 0), h).wait_recv()

    def w3_copy(d, i):
        blk = wf.at[core, chip_from(d), (wi + near[i]) % 4]
        return rcopy(blk, blk, w3s.at[d, i], w3r.at[d, i], c * 2 + (core + 1) % 2, h)

    right, left, across = (1, 0), (-1, 0), (0, 1)
    relays = (
        (((1, 0), (right,)), ((4, 0), (right, left))),
        (((1, 1), (across,)), ((3, 1), (left,)), ((4, 1), (left,))),
        (((1, 2), (across,)), ((3, 2), (left,)), ((4, 2), (left,)),
         ((1, 3), (across,)), ((3, 3), (left, across)), ((7, 0), (left,))),
        (((7, 1), (left,)), ((2, 2), (across,)), ((2, 3), (across,))),
    )
    seen = set()

    def relay(step):
        for (d, i), targets in relays[step]:
            w2_wait(d, i)
            seen.add((d, i))
            for to in targets:
                w2_send(d, i, to).start()
            w3_copy(d, i).start()

    def w2_first(k):
        blk = wf.at[core, c, (wi + near[k]) % 4]
        pltpu.make_async_copy(blk, blk, w1r.at[(wi + near[k]) % 4]).wait()
        for to in (right, left, across):
            w2_send(0, k, to).start()
        w3_copy(0, k).start()

    rhs[pl.ds(W1, TOK), pl.ds(0, DH)] = k_ref[...]
    vaug[pl.ds(W1, TOK), pl.ds(0, DH)] = v_ref[...]
    vaug[:, pl.ds(DH, DH)] = jnp.ones((KSPAN, DH), BF16)
    for hd in range(HL):
        qf[hd] = q_ref[:, hd * DH:(hd + 1) * DH].astype(F32)
    pkf[pl.ds(W2, TOK), :] = pk_ref[...].astype(F32)
    pvf[pl.ds(W2, TOK), :] = pv_ref[...].astype(F32)
    for o in range(1, 5):
        @pl.when(s < o)
        def _():
            rhs[pl.ds((4 - o) * TOK, TOK), pl.ds(0, DH)] = jnp.zeros((TOK, DH), BF16)
            vaug[pl.ds((4 - o) * TOK, TOK), pl.ds(0, DH)] = jnp.zeros((TOK, DH), BF16)
            if o == 1:
                pkc[...] = jnp.zeros((W2, DH), BF16)
                pvc[...] = jnp.zeros((W2, DH), BF16)

    w2_first(0)
    w2_first(1)
    for o in range(1, 5):
        @pl.when(s >= o)
        def _():
            for cp in halo(o):
                cp.wait_recv()
    w2_first(2)

    pkf[pl.ds(0, W2), :] = pkc[...].astype(F32)
    pvf[pl.ds(0, W2), :] = pvc[...].astype(F32)

    scale = math.log2(math.e) / math.sqrt(DH)
    lane = lax.broadcasted_iota(jnp.int32, (W2, DH), 1)
    orow = lax.broadcasted_iota(jnp.int32, (W2, DH), 0)

    def a_copy(n, kz):
        rows = pl.ds(n * 32, 32)
        return rcopy(
            abuf.at[z, rows], abuf.at[z, rows], a_s.at[n, kz], a_r.at[n, kz],
            s, ((z + kz) % NZ) * NY + yh)

    def attend(n):
        y = (yh + 1 + n) % NY
        tstar = 4 * ((y + 1) % NY)
        u = lax.broadcasted_iota(jnp.int32, (KSPAN, DH), 0)
        t = lax.broadcasted_iota(jnp.int32, (KSPAN, DH), 1)
        low = jnp.maximum(t + 1, fkrow_ref[...] - base + W1)
        ok = (u >= low) & (u <= t + W1) & (t != tstar)
        rhs[:, pl.ds(DH, DH)] = jnp.where(ok, 0.0, BIG).astype(BF16)

        def sub(i, carry):
            for j in range(SUB):
                tok = 16 * (2 * i + j // 4) + 4 * y + j % 4
                win = pkf[pl.ds(tok + 1, W2), :]
                bad = fks_ref[tok] - (base + tok) + (W2 - 1)
                hot = jnp.where((lane == tok) | ((lane == tstar) & (orow < bad)), 1.0, 0.0).astype(BF16)
                for hd in range(HL):
                    row = (j * HL + hd) * W2
                    qrow = qf[hd, pl.ds(tok, 1), :]
                    lhs[pl.ds(row, W2), pl.ds(0, DH)] = (win * qrow).astype(BF16)
                    lhs[pl.ds(row, W2), pl.ds(DH, DH)] = hot
            sc = lax.dot_general(
                lhs[...], rhs[...], (((1,), (1,)), ((), ())), preferred_element_type=F32)
            for g in range(SUB * HL):
                part = sc[g * W2:(g + 1) * W2]
                top = part[:, 0:128]
                for b in range(1, 5):
                    top = jnp.maximum(top, part[:, b * 128:(b + 1) * 128])
                top = jnp.maximum(jnp.maximum(top[0:8], top[8:16]), jnp.maximum(top[16:24], top[24:32]))
                top = jnp.max(jnp.max(top, axis=0, keepdims=True), axis=1, keepdims=True)
                prob[pl.ds(g * W2, W2), :] = jnp.exp2((part - top) * scale).astype(BF16)
            car = jnp.dot(prob[...], vaug[...], preferred_element_type=F32)
            for j in range(SUB):
                tok = 16 * (2 * i + j // 4) + 4 * y + j % 4
                win = pvf[pl.ds(tok + 1, W2), :]
                for hd in range(HL):
                    row = (j * HL + hd) * W2
                    num = car[row:row + W2, 0:DH] * win
                    den = car[row:row + W2, DH:2 * DH]
                    num = (num[0:8] + num[8:16]) + (num[16:24] + num[24:32])
                    den = (den[0:8] + den[8:16]) + (den[16:24] + den[24:32])
                    num = jnp.sum(num, axis=0, keepdims=True)
                    den = jnp.sum(den, axis=0, keepdims=True)
                    att[hd, pl.ds(i * SUB + j, 1), :] = num / den
            return carry

        lax.fori_loop(0, 32 // SUB, sub, 0, unroll=True)
        for hd in range(HL):
            abuf[z, pl.ds(n * 32, 32), pl.ds(hd * DH, DH)] = att[hd].astype(BF16)
        for kz in (4, 3, 5, 2, 6, 1, 7):
            a_copy(n, kz).start()

    for n in range(4):
        attend(n)
        if n == 0:
            w2_first(3)
        relay(n)

    for n in range(4):
        for kz in range(1, NZ):
            a_copy(n, kz).wait_recv()

    groups = ((0, 2), (2, 3), (3, 4))

    def f_copy(g, n, kz):
        lo, hi = groups[g]
        part = pl.ds(lo, hi - lo)
        return rcopy(
            fsend.at[n, (z + kz) % NZ, part], frecv.at[n, kz, part],
            f_s.at[g, n, kz], f_r.at[g, n, kz],
            s, ((z + kz) % NZ) * NY + (yh + 1 + n) % NY)

    def hops(peer):
        n, kz = peer
        return min(kz, NZ - kz) + (0, 2, 4, 2)[(n + 1) % NY]

    peers = tuple(sorted(
        ((n, kz) for n in range(4) for kz in range(NZ) if (n, kz) != (3, 0)), key=hops, reverse=True))

    order = (0, 1, 3, 4, 2, 7, 5, 6)

    def columns(pair):
        ds = order[2 * pair:2 * pair + 2]
        for d in ds:
            if d > 0:
                for i in range(4):
                    if (d, i) not in seen:
                        w2_wait(d, i)
                        w3_copy(d, i).start()
        for d in ds:
            for i in range(4):
                w3_copy(d, i).wait_recv()
        acc = None
        for zz in range(NZ):
            rhs_w = jnp.concatenate([wf[zz % 2, chip_from(d), zz // 2] for d in ds], axis=1)
            term = jnp.dot(abuf[zz], rhs_w, preferred_element_type=F32)
            acc = term if acc is None else acc + term
        for n in range(4):
            for e in range(2):
                for zz in range(NZ):
                    row = n * 32 + zz * 4
                    ffin[n, zz, pair, pl.ds(e * 4, 4), :] = acc[row:row + 4, e * 128:(e + 1) * 128]

    def push(g):
        lo, hi = groups[g]
        for n in range(4):
            fsend[n, :, lo:hi] = ffin[n, :, lo:hi].astype(BF16)
        for n, kz in peers:
            f_copy(g, n, kz).start()

    def place(g, kz):
        lo, hi = groups[g]
        total = ffin[3, z, lo:hi] if kz == 0 else None
        for n in range(4):
            if (n, kz) in peers:
                f_copy(g, n, kz).wait_recv()
                term = frecv[n, kz, lo:hi].astype(F32)
                total = term if total is None else total + term
        zs = (z + NZ - kz) % NZ
        for pair in range(lo, hi):
            for e in range(2):
                col = chip_from(order[2 * pair + e]) * (NZ * 128) + zs * 128
                out_ref[:, pl.ds(pl.multiple_of(col, 128), 128)] = total[pair - lo, e * 4:e * 4 + 4]

    for g in range(3):
        for pair in range(*groups[g]):
            columns(pair)
        push(g)
    for g in range(3):
        for kz in range(NZ):
            place(g, kz)

    for o in range(1, 5):
        @pl.when(s + o < 16)
        def _():
            for cp in halo(o):
                cp.wait_send()
    for k in range(4):
        src, dst, zd = w1_copy(k)

        @pl.when(jnp.logical_not((zd == z) & (ki == core)))
        def _():
            rcopy(src, dst, w1s.at[k], w1r.at[wi], c * 2 + ki, zd * NY + yh).wait_send()
    for i in range(4):
        for to in (right, left, across):
            w2_send(0, i, to).wait_send()
    for step in relays:
        for (d, i), targets in step:
            for to in targets:
                w2_send(d, i, to).wait_send()
    for d in range(NC):
        for i in range(4):
            w3_copy(d, i).wait_send()
    for n in range(4):
        for kz in range(1, NZ):
            a_copy(n, kz).wait_send()
    for g in range(3):
        for n, kz in peers:
            f_copy(g, n, kz).wait_send()


def local(queries, key_rows, value_rows, pair_keys, pair_values, first_key, residual, out_weight):
    vm = pl.BlockSpec(memory_space=pltpu.VMEM)
    dma = pltpu.SemaphoreType.DMA
    summed = pl.pallas_call(
        kernel,
        out_shape=jax.ShapeDtypeStruct((4, 8192), F32),
        in_specs=[vm, vm, vm, vm, vm, vm, pl.BlockSpec(memory_space=pltpu.SMEM),
                  pl.BlockSpec(memory_space=pl.ANY)],
        out_specs=vm,
        scratch_shapes=[
            pltpu.VMEM((KSPAN, 2 * DH), BF16),
            pltpu.VMEM((KSPAN, 2 * DH), BF16),
            pltpu.VMEM((W2, DH), BF16),
            pltpu.VMEM((W2, DH), BF16),
            pltpu.VMEM((W2 + TOK, DH), F32),
            pltpu.VMEM((W2 + TOK, DH), F32),
            pltpu.VMEM((HL, TOK, DH), F32),
            pltpu.VMEM((SUB * HL * W2, 2 * DH), BF16),
            pltpu.VMEM((SUB * HL * W2, KSPAN), BF16),
            pltpu.VMEM((HL, 32, DH), F32),
            pltpu.VMEM((NZ, TOK, HL * DH), BF16),
            pltpu.VMEM((2, NC, 4, HL * DH, 128), BF16),
            pltpu.VMEM((4, NZ, 4, 8, 128), F32),
            pltpu.VMEM((4, NZ, 4, 8, 128), BF16),
            pltpu.VMEM((4, NZ, 4, 8, 128), BF16),
            dma((8, 2)), dma((5, 2)),
            dma((4,)), dma((4,)),
            dma((NC, 4)), dma((NC, 4)),
            dma((NC, 4)), dma((NC, 4)),
            dma((4, NZ)), dma((4, NZ)),
            dma((3, 4, NZ)), dma((3, 4, NZ)),
        ],
        compiler_params=pltpu.CompilerParams(collective_id=0, has_side_effects=True),
        name="layer",
    )(queries, key_rows, value_rows, pair_keys, pair_values, first_key.reshape(1, TOK), first_key, out_weight)
    return residual + summed


def solution(mesh):
    placed = (
        P("seq", "head"),
        P("seq", None),
        P("seq", None),
        P("seq", None),
        P("seq", None),
        P("seq"),
        P(("seq", "head"), None),
        P("head", "seq"),
    )
    return jax.shard_map(
        local, mesh=mesh, in_specs=placed, out_specs=P(("seq", "head"), None), check_vma=False
    )
```

```python
import functools
import math

import jax
import jax.numpy as jnp
from jax import lax
from jax.experimental import pallas as pl
from jax.experimental.pallas import tpu as pltpu
from jax.sharding import PartitionSpec as P

DH = 128
W1 = 512
W2 = 32
TOK = 128
HL = 2
KSPAN = W1 + TOK
NX = 4
NZ = 8
NY = 4
NC = 8
BIG = -1e30
MESH = pl.DeviceIdType.MESH
F32 = jnp.float32
BF16 = jnp.bfloat16
SUB = 8


def kernel(
    q_ref, k_ref, v_ref, pk_ref, pv_ref, fkrow_ref, fks_ref, w_ref, out_ref,
    rhs, vaug, pkc, pvc, pkf, pvf, qf, lhs, prob, att, abuf, wf,
    ffin, fsend, frecv,
    hs, hr, w1s, w1r, w2s, w2r, w3s, w3r, a_s, a_r, f_s, f_r,
):
    s = lax.axis_index("seq")
    h = lax.axis_index("head")
    z = h // NY
    yh = h % NY
    core = s % 2
    c = s // 2
    x = c % NX
    yl = c // NX
    base = s * TOK

    def dev(seq, head):
        return {"seq": seq, "head": head}

    def rcopy(src, dst, ssem, rsem, seq, head):
        return pltpu.make_async_remote_copy(
            src_ref=src, dst_ref=dst, send_sem=ssem, recv_sem=rsem,
            device_id=dev(seq, head), device_id_type=MESH,
        )

    bar = pltpu.get_barrier_semaphore()
    count = 0
    for k in range(1, 16):
        pl.semaphore_signal(bar, inc=1, device_id=dev((s + k) % 16, h), device_id_type=MESH)
        count += 1
    for k in range(1, NZ):
        for dc in range(2):
            pl.semaphore_signal(
                bar, inc=1, device_id=dev(c * 2 + (core + dc) % 2, ((z + k) % NZ) * NY + yh),
                device_id_type=MESH)
            count += 1
    for k in range(1, NY):
        pl.semaphore_signal(bar, inc=1, device_id=dev(s, z * NY + (yh + k) % NY), device_id_type=MESH)
        count += 1
    pl.semaphore_wait(bar, count)

    def halo(o):
        rows = pl.ds((4 - o) * TOK, TOK)
        res = [
            rcopy(k_ref, rhs.at[rows, pl.ds(0, DH)], hs.at[o, 0], hr.at[o, 0], (s + o) % 16, h),
            rcopy(v_ref, vaug.at[rows, pl.ds(0, DH)], hs.at[o, 1], hr.at[o, 1], (s + o) % 16, h),
        ]
        if o == 1:
            tail = pl.ds(TOK - W2, W2)
            head = pl.ds(0, W2)
            res.append(rcopy(pk_ref.at[tail], pkc.at[head], hs.at[0, 0], hr.at[0, 0], (s + 1) % 16, h))
            res.append(rcopy(pv_ref.at[tail], pvc.at[head], hs.at[0, 1], hr.at[0, 1], (s + 1) % 16, h))
        return res

    for o in range(1, 5):
        @pl.when(s + o < 16)
        def _():
            for cp in halo(o):
                cp.start()

    near = (0, 1, 3, 2)
    ki = z % 2
    wi = z // 2

    def w1_copy(k):
        q = (z + near[k]) % 4
        src = w_ref.at[:, pl.ds(pl.multiple_of(q * 128, 128), 128)]
        dst = wf.at[ki, c, wi]
        return src, dst, 4 * core + q

    for k in range(4):
        src, dst, zd = w1_copy(k)
        mine = (zd == z) & (ki == core)

        @pl.when(mine)
        def _():
            pltpu.make_async_copy(src, dst, w1r.at[wi]).start()

        @pl.when(jnp.logical_not(mine))
        def _():
            rcopy(src, dst, w1s.at[k], w1r.at[wi], c * 2 + ki, zd * NY + yh).start()

    def chip_from(d):
        return ((yl + d // NX) % 2) * NX + (x + NX - d % NX) % NX

    def seq_at(dx, dy):
        return (((yl + dy) % 2) * NX + (x + NX + dx) % NX) * 2 + core

    def w2_send(d, i, to):
        dx, dy = to
        e = ((d // NX + dy) % 2) * NX + (d % NX + dx) % NX
        blk = wf.at[core, chip_from(d), (wi + near[i]) % 4]
        return rcopy(blk, blk, w2s.at[e, i], w2r.at[e, i], seq_at(dx, dy), h)

    def w2_wait(d, i):
        blk = wf.at[core, chip_from(d), (wi + near[i]) % 4]
        rcopy(blk, blk, w2s.at[d, i], w2r.at[d, i], seq_at(1, 0), h).wait_recv()

    def w3_copy(d, i):
        blk = wf.at[core, chip_from(d), (wi + near[i]) % 4]
        return rcopy(blk, blk, w3s.at[d, i], w3r.at[d, i], c * 2 + (core + 1) % 2, h)

    right, left, across = (1, 0), (-1, 0), (0, 1)
    relays = (
        (((3, 0), (left,)), ((4, 0), (right, left))),
        (((1, 1), (across,)), ((3, 1), (left,)), ((4, 1), (left,))),
        (((1, 2), (across,)), ((3, 2), (left,)), ((4, 2), (left,)),
         ((1, 3), (across,)), ((3, 3), (left, across)), ((7, 0), (left,))),
        (((7, 1), (left,)), ((2, 2), (across,)), ((2, 3), (across,))),
    )
    seen = set()

    def relay(step):
        for (d, i), targets in relays[step]:
            w2_wait(d, i)
            seen.add((d, i))
            for to in targets:
                w2_send(d, i, to).start()
            w3_copy(d, i).start()

    def w2_first(k):
        blk = wf.at[core, c, (wi + near[k]) % 4]
        pltpu.make_async_copy(blk, blk, w1r.at[(wi + near[k]) % 4]).wait()
        for to in (right, left, across):
            w2_send(0, k, to).start()
        w3_copy(0, k).start()

    rhs[pl.ds(W1, TOK), pl.ds(0, DH)] = k_ref[...]
    vaug[pl.ds(W1, TOK), pl.ds(0, DH)] = v_ref[...]
    vaug[:, pl.ds(DH, DH)] = jnp.ones((KSPAN, DH), BF16)
    for hd in range(HL):
        qf[hd] = q_ref[:, hd * DH:(hd + 1) * DH].astype(F32)
    pkf[pl.ds(W2, TOK), :] = pk_ref[...].astype(F32)
    pvf[pl.ds(W2, TOK), :] = pv_ref[...].astype(F32)
    for o in range(1, 5):
        @pl.when(s < o)
        def _():
            rhs[pl.ds((4 - o) * TOK, TOK), pl.ds(0, DH)] = jnp.zeros((TOK, DH), BF16)
            vaug[pl.ds((4 - o) * TOK, TOK), pl.ds(0, DH)] = jnp.zeros((TOK, DH), BF16)
            if o == 1:
                pkc[...] = jnp.zeros((W2, DH), BF16)
                pvc[...] = jnp.zeros((W2, DH), BF16)

    w2_first(0)
    w2_first(1)
    for o in range(1, 5):
        @pl.when(s >= o)
        def _():
            for cp in halo(o):
                cp.wait_recv()
    w2_first(2)

    pkf[pl.ds(0, W2), :] = pkc[...].astype(F32)
    pvf[pl.ds(0, W2), :] = pvc[...].astype(F32)

    scale = math.log2(math.e) / math.sqrt(DH)
    lane = lax.broadcasted_iota(jnp.int32, (W2, DH), 1)
    orow = lax.broadcasted_iota(jnp.int32, (W2, DH), 0)

    def a_copy(n, kz):
        rows = pl.ds(n * 32, 32)
        return rcopy(
            abuf.at[z, rows], abuf.at[z, rows], a_s.at[n, kz], a_r.at[n, kz],
            s, ((z + kz) % NZ) * NY + yh)

    def attend(n):
        y = (yh + 1 + n) % NY
        tstar = 4 * ((y + 1) % NY)
        u = lax.broadcasted_iota(jnp.int32, (KSPAN, DH), 0)
        t = lax.broadcasted_iota(jnp.int32, (KSPAN, DH), 1)
        low = jnp.maximum(t + 1, fkrow_ref[...] - base + W1)
        ok = (u >= low) & (u <= t + W1) & (t != tstar)
        rhs[:, pl.ds(DH, DH)] = jnp.where(ok, 0.0, BIG).astype(BF16)

        def sub(i, carry):
            for j in range(SUB):
                tok = 16 * (2 * i + j // 4) + 4 * y + j % 4
                win = pkf[pl.ds(tok + 1, W2), :]
                bad = fks_ref[tok] - (base + tok) + (W2 - 1)
                hot = jnp.where((lane == tok) | ((lane == tstar) & (orow < bad)), 1.0, 0.0).astype(BF16)
                for hd in range(HL):
                    row = (j * HL + hd) * W2
                    qrow = qf[hd, pl.ds(tok, 1), :]
                    lhs[pl.ds(row, W2), pl.ds(0, DH)] = (win * qrow).astype(BF16)
                    lhs[pl.ds(row, W2), pl.ds(DH, DH)] = hot
            sc = lax.dot_general(
                lhs[...], rhs[...], (((1,), (1,)), ((), ())), preferred_element_type=F32)
            for g in range(SUB * HL):
                part = sc[g * W2:(g + 1) * W2]
                top = part[:, 0:128]
                for b in range(1, 5):
                    top = jnp.maximum(top, part[:, b * 128:(b + 1) * 128])
                top = jnp.maximum(jnp.maximum(top[0:8], top[8:16]), jnp.maximum(top[16:24], top[24:32]))
                top = jnp.max(jnp.max(top, axis=0, keepdims=True), axis=1, keepdims=True)
                prob[pl.ds(g * W2, W2), :] = jnp.exp2((part - top) * scale).astype(BF16)
            car = jnp.dot(prob[...], vaug[...], preferred_element_type=F32)
            for j in range(SUB):
                tok = 16 * (2 * i + j // 4) + 4 * y + j % 4
                win = pvf[pl.ds(tok + 1, W2), :]
                for hd in range(HL):
                    row = (j * HL + hd) * W2
                    num = car[row:row + W2, 0:DH] * win
                    den = car[row:row + W2, DH:2 * DH]
                    num = (num[0:8] + num[8:16]) + (num[16:24] + num[24:32])
                    den = (den[0:8] + den[8:16]) + (den[16:24] + den[24:32])
                    num = jnp.sum(num, axis=0, keepdims=True)
                    den = jnp.sum(den, axis=0, keepdims=True)
                    att[hd, pl.ds(i * SUB + j, 1), :] = num / den
            return carry

        lax.fori_loop(0, 32 // SUB, sub, 0, unroll=True)
        for hd in range(HL):
            abuf[z, pl.ds(n * 32, 32), pl.ds(hd * DH, DH)] = att[hd].astype(BF16)
        for kz in (4, 3, 5, 2, 6, 1, 7):
            a_copy(n, kz).start()

    for n in range(4):
        attend(n)
        if n == 0:
            w2_first(3)
        relay(n)

    for n in range(4):
        for kz in range(1, NZ):
            a_copy(n, kz).wait_recv()

    groups = ((0, 2), (2, 3), (3, 4))

    def f_copy(g, n, kz):
        lo, hi = groups[g]
        part = pl.ds(lo, hi - lo)
        return rcopy(
            fsend.at[n, (z + kz) % NZ, part], frecv.at[n, kz, part],
            f_s.at[g, n, kz], f_r.at[g, n, kz],
            s, ((z + kz) % NZ) * NY + (yh + 1 + n) % NY)

    def hops(peer):
        n, kz = peer
        return min(kz, NZ - kz) + (0, 2, 4, 2)[(n + 1) % NY]

    peers = tuple(sorted(
        ((n, kz) for n in range(4) for kz in range(NZ) if (n, kz) != (3, 0)), key=hops, reverse=True))

    order = (0, 1, 3, 4, 2, 7, 5, 6)

    def columns(pair):
        ds = order[2 * pair:2 * pair + 2]
        for d in ds:
            if d > 0:
                for i in range(4):
                    if (d, i) not in seen:
                        w2_wait(d, i)
                        w3_copy(d, i).start()
        for d in ds:
            for i in range(4):
                w3_copy(d, i).wait_recv()
        acc = None
        for zz in range(NZ):
            rhs_w = jnp.concatenate([wf[zz % 2, chip_from(d), zz // 2] for d in ds], axis=1)
            term = jnp.dot(abuf[zz], rhs_w, preferred_element_type=F32)
            acc = term if acc is None else acc + term
        for n in range(4):
            for e in range(2):
                for zz in range(NZ):
                    row = n * 32 + zz * 4
                    ffin[n, zz, pair, pl.ds(e * 4, 4), :] = acc[row:row + 4, e * 128:(e + 1) * 128]

    def push(g):
        lo, hi = groups[g]
        for n in range(4):
            fsend[n, :, lo:hi] = ffin[n, :, lo:hi].astype(BF16)
        for n, kz in peers:
            f_copy(g, n, kz).start()

    def place(g, kz):
        lo, hi = groups[g]
        total = ffin[3, z, lo:hi] if kz == 0 else None
        for n in range(4):
            if (n, kz) in peers:
                f_copy(g, n, kz).wait_recv()
                term = frecv[n, kz, lo:hi].astype(F32)
                total = term if total is None else total + term
        zs = (z + NZ - kz) % NZ
        for pair in range(lo, hi):
            for e in range(2):
                col = chip_from(order[2 * pair + e]) * (NZ * 128) + zs * 128
                out_ref[:, pl.ds(pl.multiple_of(col, 128), 128)] = total[pair - lo, e * 4:e * 4 + 4]

    for g in range(3):
        for pair in range(*groups[g]):
            columns(pair)
        push(g)
    for g in range(3):
        for kz in range(NZ):
            place(g, kz)

    for o in range(1, 5):
        @pl.when(s + o < 16)
        def _():
            for cp in halo(o):
                cp.wait_send()
    for k in range(4):
        src, dst, zd = w1_copy(k)

        @pl.when(jnp.logical_not((zd == z) & (ki == core)))
        def _():
            rcopy(src, dst, w1s.at[k], w1r.at[wi], c * 2 + ki, zd * NY + yh).wait_send()
    for i in range(4):
        for to in (right, left, across):
            w2_send(0, i, to).wait_send()
    for step in relays:
        for (d, i), targets in step:
            for to in targets:
                w2_send(d, i, to).wait_send()
    for d in range(NC):
        for i in range(4):
            w3_copy(d, i).wait_send()
    for n in range(4):
        for kz in range(1, NZ):
            a_copy(n, kz).wait_send()
    for g in range(3):
        for n, kz in peers:
            f_copy(g, n, kz).wait_send()


def local(queries, key_rows, value_rows, pair_keys, pair_values, first_key, residual, out_weight):
    vm = pl.BlockSpec(memory_space=pltpu.VMEM)
    dma = pltpu.SemaphoreType.DMA
    summed = pl.pallas_call(
        kernel,
        out_shape=jax.ShapeDtypeStruct((4, 8192), F32),
        in_specs=[vm, vm, vm, vm, vm, vm, pl.BlockSpec(memory_space=pltpu.SMEM),
                  pl.BlockSpec(memory_space=pl.ANY)],
        out_specs=vm,
        scratch_shapes=[
            pltpu.VMEM((KSPAN, 2 * DH), BF16),
            pltpu.VMEM((KSPAN, 2 * DH), BF16),
            pltpu.VMEM((W2, DH), BF16),
            pltpu.VMEM((W2, DH), BF16),
            pltpu.VMEM((W2 + TOK, DH), F32),
            pltpu.VMEM((W2 + TOK, DH), F32),
            pltpu.VMEM((HL, TOK, DH), F32),
            pltpu.VMEM((SUB * HL * W2, 2 * DH), BF16),
            pltpu.VMEM((SUB * HL * W2, KSPAN), BF16),
            pltpu.VMEM((HL, 32, DH), F32),
            pltpu.VMEM((NZ, TOK, HL * DH), BF16),
            pltpu.VMEM((2, NC, 4, HL * DH, 128), BF16),
            pltpu.VMEM((4, NZ, 4, 8, 128), F32),
            pltpu.VMEM((4, NZ, 4, 8, 128), BF16),
            pltpu.VMEM((4, NZ, 4, 8, 128), BF16),
            dma((8, 2)), dma((5, 2)),
            dma((4,)), dma((4,)),
            dma((NC, 4)), dma((NC, 4)),
            dma((NC, 4)), dma((NC, 4)),
            dma((4, NZ)), dma((4, NZ)),
            dma((3, 4, NZ)), dma((3, 4, NZ)),
        ],
        compiler_params=pltpu.CompilerParams(collective_id=0, has_side_effects=True),
        name="layer",
    )(queries, key_rows, value_rows, pair_keys, pair_values, first_key.reshape(1, TOK), first_key, out_weight)
    return residual + summed


def solution(mesh):
    placed = (
        P("seq", "head"),
        P("seq", None),
        P("seq", None),
        P("seq", None),
        P("seq", None),
        P("seq"),
        P(("seq", "head"), None),
        P("head", "seq"),
    )
    return jax.shard_map(
        local, mesh=mesh, in_specs=placed, out_specs=P(("seq", "head"), None), check_vma=False
    )
```
